32 devices in a mesh: row: 4 (over y, x), col: 8 (over z, core).
Axes of the slice: x: 2, y: 2, z: 4, core: 2. Of those that a mesh axis runs over, the one named last changes fastest.
Arguments:
- schur: float32 [8192, 8192], P('row', 'col'), may hold values from -6 to 6
- panel_raw: bfloat16 [8192, 1024], P('col', 'row'), may hold values from -0.59765625 to 0.59765625
- diag_inverse: bfloat16 [1024, 1024], replicated, may hold values from -1 to 2, as said below
- perm: int32 [64], replicated, may hold values from 0 to 63, as said below
- pattern: int32 [64, 64], P('row', 'col'), may hold values 0 or 1
Outputs:
- schur_out: float32 [8192, 8192], P('row', 'col')
The draws below stay inside these ranges and needn't reach their ends.
Inputs may be any that keep to these rules, and one draw needn't show every extreme that they name: diag_inverse is lower triangular with diagonal entries between 0.5 and 2. perm names every block row once. Holder h holds the owner-order blocks h * 8 to (h + 1) * 8 - 1; a column group is a run of 8 consecutive global block rows starting at a multiple of it. The blocks of one holder fall into the column groups as evenly as possible: at most 1 into one group, and exactly 1 into some group.
All inputs are finite; a program needn't handle non-finite values. No bound on the sum of `pattern` on one device may be relied on, other than what follows from the above.
Results may differ from the reference program's by a relative error of at most 0.007.
Values may be sent and summed in bfloat16 or wider, within the bound.
A program may use at most 192 MiB of HBM per device.

```python
import jax
import jax.numpy as jnp
from jax import lax

BLK = 128
SNW = 1024
NB = 64
OWNERS = 8


def draw_diag_inverse(key, part):
    key_off = jax.random.fold_in(key, 11)
    key_diag = jax.random.fold_in(key, 12)
    indices = jnp.arange(SNW, dtype=jnp.int32)
    below = indices[:, None] > indices[None, :]
    on_diag = indices[:, None] == indices[None, :]
    spread = 0.5 / jnp.sqrt(jnp.float32(SNW))
    off_part = jax.random.truncated_normal(key_off, -3.0, 3.0, (SNW, SNW), jnp.float32) * spread
    diag_part = jnp.exp(jax.random.uniform(key_diag, (SNW,), jnp.float32, -0.69, 0.69))
    result = jnp.where(below, off_part, 0.0) + jnp.where(on_diag, diag_part[None, :], 0.0)
    return result.astype(jnp.bfloat16)


def shuffle_rows(base_key, count, length):
    subkeys = jax.random.split(base_key, count)
    return jax.vmap(lambda subkey: jax.random.permutation(subkey, length))(subkeys)


def draw_perm(key, part):
    own_count = NB // OWNERS
    key_offsets = jax.random.fold_in(key, 21)
    key_labels = jax.random.fold_in(key, 22)
    key_within = jax.random.fold_in(key, 23)
    key_orders = jax.random.fold_in(key, 24)
    offsets = jax.random.permutation(key_offsets, OWNERS)
    labels = jax.random.permutation(key_labels, OWNERS)
    step_ids = jnp.arange(own_count, dtype=jnp.int32)
    groups = labels[(offsets[:, None] + step_ids[None, :]) % OWNERS]
    within = shuffle_rows(key_within, OWNERS, own_count)
    target = groups * own_count + within[groups, step_ids[None, :]]
    orders = shuffle_rows(key_orders, OWNERS, own_count)
    return jnp.take_along_axis(target, orders, axis=1).reshape(NB).astype(jnp.int32)


def plant(array, own_key, low, largest):
    index_at = [jax.random.randint(jax.random.fold_in(own_key, axis), (), 0, length) for axis, length in enumerate(array.shape)]
    longest = array.shape.index(max(array.shape))
    neighbour = index_at[:longest] + [(index_at[longest] + 1) % array.shape[longest]] + index_at[longest + 1:]
    return array.at[tuple(index_at)].set(low).at[tuple(neighbour)].set(largest)


def block_scale(key, extent, shards, low, top_value):
    def one(dim, blocks):
        steps = jax.random.uniform(jax.random.fold_in(jax.random.fold_in(key, 6), dim), (blocks,), jnp.float32, low / len(shards), top_value / len(shards))
        return jnp.repeat(jnp.exp(steps), extent[dim] // blocks).reshape((-1,) + (1,) * (len(extent) - dim - 1))

    factor_of = one(*shards[0])
    for cut in shards[1:]:
        factor_of = factor_of * one(*cut)
    return factor_of


def gaussian(key, shape, deviation, limit, cuts=(), held_as=jnp.bfloat16):
    loudness = block_scale(key, shape, cuts, -0.22, 0.18) if cuts else 1.0
    entries = jax.random.normal(key, shape, jnp.float32) * deviation * loudness
    return jnp.minimum(jnp.maximum(entries, -limit), limit).astype(held_as)


def setup_inputs(seed: int = 0) -> dict:
    key_list = jax.random.split(jax.random.key(seed), 6)
    return {
        "schur": gaussian(key_list[0], (NB * BLK, NB * BLK), 1.0, 6.0, ((0, 4), (1, 8)), jnp.float32),
        "panel_raw": gaussian(key_list[1], (NB * BLK, SNW), 0.1, 0.59765625, ((0, 8), (1, 4))),
        "diag_inverse": draw_diag_inverse(jax.random.fold_in(key_list[5], 71), 0),
        "perm": draw_perm(jax.random.fold_in(key_list[5], 71), 0),
        "pattern": plant((jax.random.randint(key_list[4], (NB, NB), 0, 2) < 1).astype(jnp.int32), jax.random.fold_in(key_list[4], 1), 0, 1),
    }


def reference(schur, panel_raw, diag_inverse, perm, pattern):
    owned = lax.dot_general(panel_raw, diag_inverse, (((1,), (1,)), ((), ())), preferred_element_type=jnp.float32).astype(jnp.bfloat16)
    position = jnp.zeros((NB,), jnp.int32).at[perm].set(jnp.arange(NB, dtype=jnp.int32))
    panel = owned.reshape(NB, BLK, SNW)[position].reshape(NB * BLK, SNW)

    def one_row(inputs):
        rows_now, mask_row, panel_row = inputs
        update = lax.dot_general(panel_row, panel, (((1,), (1,)), ((), ())), preferred_element_type=jnp.float32)
        weight = jnp.repeat(mask_row.astype(jnp.float32), BLK, total_repeat_length=NB * BLK)
        return rows_now - update * weight[None, :]

    result = lax.map(one_row, (schur.reshape(NB, BLK, NB * BLK), pattern, panel.reshape(NB, BLK, SNW)))
    return result.reshape(NB * BLK, NB * BLK)
```

```python
import functools

import jax
import jax.numpy as jnp
from jax import lax
from jax.experimental import pallas as pl
from jax.experimental.pallas import tpu as pltpu
from jax.sharding import PartitionSpec as P

BLK = 128
MESH = pl.DeviceIdType.MESH


def times_inverse(left, right):
    return lax.dot_general(
        left, right, (((1,), (1,)), ((), ())), preferred_element_type=jnp.float32
    )


def exchange_kernel(
    n_row, n_col, gpr,
    src_ref, raw_ref, d_hbm, rows_ref, cpan_ref,
    sorted_ref, a_ref, b_ref, own_ref, d_ref,
    a_send, a_recv, b_send, b_recv, c_send, c_recv, z_send, z_recv, f_send, f_recv, loc,
):
    r = lax.axis_index("row")
    c = lax.axis_index("col")
    n_pos = n_col // 2
    pos = c // 2
    core = c % 2
    sibling = pos * 2 + (1 - core)
    kw = raw_ref.shape[2]
    load_d = pltpu.make_async_copy(d_hbm, d_ref, loc.at[0])
    load_d.start()

    def remote(src, dst, ssem, rsem, rr, cc):
        return pltpu.make_async_remote_copy(
            src_ref=src, dst_ref=dst, send_sem=ssem, recv_sem=rsem,
            device_id=(rr, cc), device_id_type=MESH,
        )

    barrier = pltpu.get_barrier_semaphore()
    for dr in range(1, n_row):
        pl.semaphore_signal(barrier, inc=1, device_id=((r + dr) % n_row, c), device_id_type=MESH)
    for dc in range(1, n_col):
        pl.semaphore_signal(barrier, inc=1, device_id=(r, (c + dc) % n_col), device_id_type=MESH)
    for g in range(n_col):
        sorted_ref[g] = raw_ref[src_ref[g]]
    pl.semaphore_wait(barrier, n_row + n_col - 2)

    def a_copy(dr):
        to = (r + dr) % n_row
        return remote(sorted_ref.at[pl.ds(to * gpr, gpr)], a_ref.at[r],
                      a_send.at[dr], a_recv.at[dr], to, c)

    def b_copy(dc):
        to = (c + dc) % n_col
        return remote(sorted_ref.at[to], b_ref.at[c], b_send.at[dc], b_recv.at[dc], r, to)

    for dr in range(1, n_row):
        a_copy(dr).start()
    for dc in range(1, n_col):
        b_copy(dc).start()
    a_ref[r] = sorted_ref[pl.ds(r * gpr, gpr)]
    b_ref[c] = sorted_ref[c]
    load_d.wait()
    for dr in range(1, n_row):
        came = (r + n_row - dr) % n_row
        remote(sorted_ref.at[pl.ds(r * gpr, gpr)], a_ref.at[came],
               a_send.at[dr], a_recv.at[dr], (r + dr) % n_row, c).wait_recv()
    total = times_inverse(a_ref[0].reshape(gpr * BLK, kw), d_ref[:, :kw])
    for s in range(1, n_row):
        total += times_inverse(a_ref[s].reshape(gpr * BLK, kw), d_ref[:, s * kw:(s + 1) * kw])
    own_ref[...] = total.astype(jnp.bfloat16).reshape(own_ref.shape)

    def z_copy(dp):
        to = (pos + dp) % n_pos
        return remote(own_ref, rows_ref.at[c], z_send.at[dp], z_recv.at[dp], r, to * 2 + core)

    for dp in range(1, n_pos):
        z_copy(dp).start()
    f_own = remote(own_ref, rows_ref.at[c], f_send.at[0], f_recv.at[0], r, sibling)
    f_own.start()
    keep = pltpu.make_async_copy(own_ref, rows_ref.at[c], loc.at[1])
    keep.start()

    for dc in range(1, n_col):
        came = (c + n_col - dc) % n_col
        remote(sorted_ref.at[0], b_ref.at[came], b_send.at[dc], b_recv.at[dc],
               r, (c + dc) % n_col).wait_recv()

    def c_copy(dr):
        return remote(b_ref, cpan_ref.at[r], c_send.at[dr], c_recv.at[dr], (r + dr) % n_row, c)

    for dr in range(1, n_row):
        c_copy(dr).start()
    keep_c = pltpu.make_async_copy(b_ref, cpan_ref.at[r], loc.at[2])
    keep_c.start()

    def f_copy(dp):
        slot = ((pos + n_pos - dp) % n_pos) * 2 + core
        return remote(rows_ref.at[slot], rows_ref.at[slot], f_send.at[dp], f_recv.at[dp], r, sibling)

    for dp in range(1, n_pos):
        slot = ((pos + n_pos - dp) % n_pos) * 2 + core
        remote(own_ref, rows_ref.at[slot], z_send.at[dp], z_recv.at[dp],
               r, ((pos + dp) % n_pos) * 2 + core).wait_recv()
        f_copy(dp).start()
    for dp in range(n_pos):
        slot = ((pos + n_pos - dp) % n_pos) * 2 + (1 - core)
        remote(own_ref, rows_ref.at[slot], f_send.at[dp], f_recv.at[dp], r, sibling).wait_recv()
    for dr in range(1, n_row):
        came = (r + n_row - dr) % n_row
        remote(b_ref, cpan_ref.at[came], c_send.at[dr], c_recv.at[dr],
               (r + dr) % n_row, c).wait_recv()
    for dr in range(1, n_row):
        a_copy(dr).wait_send()
        c_copy(dr).wait_send()
    for dc in range(1, n_col):
        b_copy(dc).wait_send()
    f_own.wait_send()
    for dp in range(1, n_pos):
        z_copy(dp).wait_send()
        f_copy(dp).wait_send()
    keep.wait()
    keep_c.wait()


def update_kernel(
    n_row, block_cols,
    rows_idx, cols_idx, low_ref, high_ref, cpan_ref, d_ref, pat_ref, schur_ref, out_ref, cols_ref,
):
    kw = cpan_ref.shape[3]

    @pl.when(pl.program_id(0) == 0)
    def _():
        for w in range(block_cols):
            h = cols_idx[w]
            total = times_inverse(cpan_ref[0, h], d_ref[:, :kw])
            for s in range(1, n_row):
                total += times_inverse(cpan_ref[s, h], d_ref[:, s * kw:(s + 1) * kw])
            cols_ref[w * BLK:(w + 1) * BLK, :] = total.astype(jnp.bfloat16)

    left = jnp.concatenate([low_ref[0, 0], high_ref[0, 0]], axis=0)
    update = times_inverse(left, cols_ref[...])
    for e in range(2):
        part = slice(e * BLK, (e + 1) * BLK)
        out_ref[part, :] = schur_ref[part, :] - update[part, :] * pat_ref[e]


def local(schur, panel_raw, diag_inverse, perm, pattern):
    n_row = lax.axis_size("row")
    n_col = lax.axis_size("col")
    r = lax.axis_index("row")
    c = lax.axis_index("col")
    local_rows, local_cols = schur.shape
    block_rows, block_cols = local_rows // BLK, local_cols // BLK
    gpr = local_rows // local_cols
    held, kw = panel_raw.shape[0] // BLK, panel_raw.shape[1]
    snw = diag_inverse.shape[0]
    blocks = perm.shape[0]
    bf16 = jnp.bfloat16

    mine = lax.dynamic_slice_in_dim(perm, c * held, held, 0)
    group_of = mine // block_cols
    at = jnp.arange(held, dtype=jnp.int32)
    groups = jnp.arange(n_col, dtype=jnp.int32)
    source = jnp.sum(jnp.where(group_of[None, :] == groups[:, None], at[None, :], 0), axis=1)
    holder = jnp.arange(blocks, dtype=jnp.int32) // held

    def holders_of(first, count):
        ids = first + jnp.arange(count, dtype=jnp.int32)
        return jnp.sum(jnp.where(perm[None, :] == ids[:, None], holder[None, :], 0), axis=1)

    rows_idx = holders_of(r * block_rows, block_rows)
    cols_idx = holders_of(c * block_cols, block_cols)
    n_pos = n_col // 2
    dma = pltpu.SemaphoreType.DMA
    rows, cpan = pl.pallas_call(
        functools.partial(exchange_kernel, n_row, n_col, gpr),
        out_shape=(
            jax.ShapeDtypeStruct((n_col, gpr, BLK, snw), bf16),
            jax.ShapeDtypeStruct((n_row, n_col, BLK, kw), bf16),
        ),
        in_specs=[
            pl.BlockSpec(memory_space=pltpu.SMEM),
            pl.BlockSpec(memory_space=pltpu.VMEM),
            pl.BlockSpec(memory_space=pl.ANY),
        ],
        out_specs=(pl.BlockSpec(memory_space=pl.ANY), pl.BlockSpec(memory_space=pl.ANY)),
        scratch_shapes=[
            pltpu.VMEM((n_col, BLK, kw), bf16),
            pltpu.VMEM((n_row, gpr, BLK, kw), bf16),
            pltpu.VMEM((n_col, BLK, kw), bf16),
            pltpu.VMEM((gpr, BLK, snw), bf16),
            pltpu.VMEM((snw, snw), bf16),
            dma((n_row,)), dma((n_row,)), dma((n_col,)), dma((n_col,)),
            dma((n_row,)), dma((n_row,)), dma((n_pos,)), dma((n_pos,)),
            dma((n_pos,)), dma((n_pos,)), dma((3,)),
        ],
        compiler_params=pltpu.CompilerParams(
            collective_id=0, has_side_effects=True, vmem_limit_bytes=32 * 2**20
        ),
    )(source, panel_raw.reshape(held, BLK, kw), diag_inverse)

    weights = jnp.repeat(pattern.astype(jnp.float32), BLK, axis=1)[:, None, :]

    def row_spec(e):
        return pl.BlockSpec(
            (1, 1, BLK, snw),
            lambda i, ri, ci: (ri[2 * i + e], (2 * i + e) // block_cols, 0, 0),
        )

    return pl.pallas_call(
        functools.partial(update_kernel, n_row, block_cols),
        out_shape=jax.ShapeDtypeStruct(schur.shape, schur.dtype),
        grid_spec=pltpu.PrefetchScalarGridSpec(
            num_scalar_prefetch=2,
            grid=(block_rows // 2,),
            in_specs=[
                row_spec(0),
                row_spec(1),
                pl.BlockSpec((n_row, n_col, BLK, kw), lambda i, ri, ci: (0, 0, 0, 0)),
                pl.BlockSpec((snw, snw), lambda i, ri, ci: (0, 0)),
                pl.BlockSpec((2, 1, local_cols), lambda i, ri, ci: (i, 0, 0)),
                pl.BlockSpec((2 * BLK, local_cols), lambda i, ri, ci: (i, 0)),
            ],
            out_specs=pl.BlockSpec((2 * BLK, local_cols), lambda i, ri, ci: (i, 0)),
            scratch_shapes=[pltpu.VMEM((local_cols, snw), bf16)],
        ),
        compiler_params=pltpu.CompilerParams(vmem_limit_bytes=40 * 2**20),
    )(rows_idx, cols_idx, rows, rows, cpan, diag_inverse, weights, schur)


def solution(mesh):
    return jax.shard_map(
        local,
        mesh=mesh,
        in_specs=(P("row", "col"), P("col", "row"), P(), P(), P("row", "col")),
        out_specs=P("row", "col"),
        check_vma=False,
    )
```

```python
import functools

import jax
import jax.numpy as jnp
from jax import lax
from jax.experimental import pallas as pl
from jax.experimental.pallas import tpu as pltpu
from jax.sharding import PartitionSpec as P

BLK = 128
MESH = pl.DeviceIdType.MESH


def times_inverse(left, right):
    return lax.dot_general(
        left, right, (((1,), (1,)), ((), ())), preferred_element_type=jnp.float32
    )


def exchange_kernel(
    n_row, n_col, gpr, held, block_cols,
    perm_ref, table_ref, raw_hbm, d_hbm, rows_ref, cols_ref,
    raw_ref, sorted_ref, a_ref, b_ref, own_ref, d_ref, cpan_ref,
    a_send, a_recv, b_send, b_recv, c_send, c_recv,
    up_send, up_recv, down_send, down_recv, f_send, f_recv, loc,
):
    r = lax.axis_index("row")
    c = lax.axis_index("col")
    n_pos = n_col // 2
    pos = c // 2
    core = c % 2
    sibling = pos * 2 + (1 - core)
    kw = raw_ref.shape[2]
    snw = d_ref.shape[0]
    load_raw = pltpu.make_async_copy(raw_hbm, raw_ref, loc.at[3])
    load_raw.start()
    load_d = pltpu.make_async_copy(d_hbm, d_ref, loc.at[0])
    load_d.start()

    def remote(src, dst, ssem, rsem, rr, cc):
        return pltpu.make_async_remote_copy(
            src_ref=src, dst_ref=dst, send_sem=ssem, recv_sem=rsem,
            device_id=(rr, cc), device_id_type=MESH,
        )

    def part(index):
        return pl.ds(pl.multiple_of(index * kw, kw), kw)

    barrier = pltpu.get_barrier_semaphore()
    for dr in range(1, n_row):
        pl.semaphore_signal(barrier, inc=1, device_id=((r + dr) % n_row, c), device_id_type=MESH)
    for dc in range(1, n_col):
        pl.semaphore_signal(barrier, inc=1, device_id=(r, (c + dc) % n_col), device_id_type=MESH)
    groups = [lax.div(perm_ref[c * held + i], block_cols) for i in range(held)]
    load_raw.wait()
    for g in range(n_col):
        block = 0
        for i in range(1, held):
            block = jnp.where(groups[i] == g, i, block)
        sorted_ref[g] = raw_ref[block]
    pl.semaphore_wait(barrier, n_row + n_col - 2)

    def a_copy(dr, came=None):
        to = (r + dr) % n_row
        return remote(sorted_ref.at[pl.ds(to * gpr, gpr)],
                      a_ref.at[:, :, part(r if came is None else came)],
                      a_send.at[dr], a_recv.at[dr], to, c)

    def b_copy(dc, came=None):
        to = (c + dc) % n_col
        return remote(sorted_ref.at[to], b_ref.at[c if came is None else came],
                      b_send.at[dc], b_recv.at[dc], r, to)

    for dr in range(1, n_row):
        a_copy(dr).start()
    for dc in range(1, n_col):
        b_copy(dc).start()
    a_ref[:, :, part(r)] = sorted_ref[pl.ds(r * gpr, gpr)]
    b_ref[c] = sorted_ref[c]
    load_d.wait()
    for dr in range(1, n_row):
        a_copy(dr, (r + n_row - dr) % n_row).wait_recv()
    own = times_inverse(a_ref[...].reshape(gpr * BLK, snw), d_ref[...])
    own_ref[...] = own.astype(jnp.bfloat16).reshape(own_ref.shape)

    def up_copy(d):
        slot = (pos - d) * 2 + core
        return remote(own_ref if d == 0 else rows_ref.at[slot], rows_ref.at[slot],
                      up_send.at[d], up_recv.at[d], r, (pos + 1) * 2 + core)

    def down_copy(d):
        slot = (pos + d) * 2 + core
        return remote(own_ref if d == 0 else rows_ref.at[slot], rows_ref.at[slot],
                      down_send.at[d], down_recv.at[d], r, (pos - 1) * 2 + core)

    def side_copy(source, mine):
        slot = source * 2 + core
        return remote(own_ref if mine else rows_ref.at[slot], rows_ref.at[slot],
                      f_send.at[source], f_recv.at[source], r, sibling)

    @pl.when(pos < n_pos - 1)
    def _():
        up_copy(0).start()

    @pl.when(pos > 0)
    def _():
        down_copy(0).start()

    side_copy(pos, True).start()
    keep = pltpu.make_async_copy(own_ref, rows_ref.at[c], loc.at[1])
    keep.start()

    for dc in range(1, n_col):
        b_copy(dc, (c + n_col - dc) % n_col).wait_recv()

    def c_copy(dr, came=None):
        return remote(b_ref, cpan_ref.at[:, :, part(r if came is None else came)],
                      c_send.at[dr], c_recv.at[dr], (r + dr) % n_row, c)

    for dr in range(1, n_row):
        c_copy(dr).start()
    cpan_ref[:, :, part(r)] = b_ref[...]

    def factor_columns():
        for dr in range(1, n_row):
            c_copy(dr, (r + n_row - dr) % n_row).wait_recv()
        step = 4 if block_cols % 4 == 0 else 1
        for w in range(0, block_cols, step):
            left = jnp.concatenate([cpan_ref[table_ref[w + k]] for k in range(step)], axis=0)
            done = times_inverse(left, d_ref[...]).astype(jnp.bfloat16)
            cols_ref[w * BLK:(w + step) * BLK, :] = done

    for d in range(1, n_pos):
        if d == n_pos - 1:
            factor_columns()

        @pl.when(pos - d >= 0)
        def _(d=d):
            slot = (pos - d) * 2 + core
            remote(own_ref, rows_ref.at[slot], up_send.at[d - 1], up_recv.at[d - 1],
                   r, sibling).wait_recv()
            if d < n_pos - 1:
                @pl.when(pos < n_pos - 1)
                def _():
                    up_copy(d).start()
            side_copy(pos - d, False).start()

        @pl.when(pos + d <= n_pos - 1)
        def _(d=d):
            slot = (pos + d) * 2 + core
            remote(own_ref, rows_ref.at[slot], down_send.at[d - 1], down_recv.at[d - 1],
                   r, sibling).wait_recv()
            if d < n_pos - 1:
                @pl.when(pos > 0)
                def _():
                    down_copy(d).start()
            side_copy(pos + d, False).start()

    for dr in range(1, n_row):
        a_copy(dr).wait_send()
        c_copy(dr).wait_send()
    for dc in range(1, n_col):
        b_copy(dc).wait_send()
    for d in range(n_pos - 1):
        @pl.when((pos - d >= 0) & (pos < n_pos - 1))
        def _(d=d):
            up_copy(d).wait_send()

        @pl.when((pos + d <= n_pos - 1) & (pos > 0))
        def _(d=d):
            down_copy(d).wait_send()
    for source in range(n_pos):
        slot = source * 2 + (1 - core)
        remote(own_ref, rows_ref.at[slot], f_send.at[source], f_recv.at[source],
               r, sibling).wait_recv()
        side_copy(source, True).wait_send()
    keep.wait()


def update_kernel(
    table, pat_ref, low_ref, high_ref, cols_ref, schur_ref, out_ref,
):
    i = pl.program_id(0)
    left = jnp.concatenate([low_ref[0, 0], high_ref[0, 0]], axis=0)
    update = times_inverse(left, cols_ref[...])
    for e in range(2):
        rows = slice(e * BLK, (e + 1) * BLK)
        for w in range(cols_ref.shape[0] // BLK):
            at = slice(w * BLK, (w + 1) * BLK)
            weight = pat_ref[2 * i + e, w].astype(jnp.float32)
            out_ref[rows, at] = schur_ref[rows, at] - update[rows, at] * weight


def local(schur, panel_raw, diag_inverse, perm, pattern):
    n_row = lax.axis_size("row")
    n_col = lax.axis_size("col")
    r = lax.axis_index("row")
    c = lax.axis_index("col")
    local_rows, local_cols = schur.shape
    block_rows, block_cols = local_rows // BLK, local_cols // BLK
    gpr = local_rows // local_cols
    held, kw = panel_raw.shape[0] // BLK, panel_raw.shape[1]
    snw = diag_inverse.shape[0]
    blocks = perm.shape[0]
    bf16 = jnp.bfloat16

    at = jnp.arange(block_cols + block_rows, dtype=jnp.int32)
    ids = jnp.where(at < block_cols, c * block_cols + at, r * block_rows + at - block_cols)
    holder = lax.div(lax.broadcasted_iota(jnp.int32, (ids.shape[0], blocks), 1), held)
    table = jnp.sum(jnp.where(perm[None, :] == ids[:, None], holder, 0), axis=1)
    n_pos = n_col // 2
    dma = pltpu.SemaphoreType.DMA
    smem = pl.BlockSpec(memory_space=pltpu.SMEM)
    hbm = pl.BlockSpec(memory_space=pltpu.HBM)
    rows, cols = pl.pallas_call(
        functools.partial(exchange_kernel, n_row, n_col, gpr, held, block_cols),
        out_shape=(
            jax.ShapeDtypeStruct((n_col, gpr, BLK, snw), bf16),
            jax.ShapeDtypeStruct((local_cols, snw), bf16),
        ),
        in_specs=[smem, smem, hbm, hbm],
        out_specs=(
            pl.BlockSpec(memory_space=pl.ANY),
            pl.BlockSpec(memory_space=pltpu.VMEM),
        ),
        scratch_shapes=[
            pltpu.VMEM((held, BLK, kw), bf16),
            pltpu.VMEM((n_col, BLK, kw), bf16),
            pltpu.VMEM((gpr, BLK, snw), bf16),
            pltpu.VMEM((n_col, BLK, kw), bf16),
            pltpu.VMEM((gpr, BLK, snw), bf16),
            pltpu.VMEM((snw, snw), bf16),
            pltpu.VMEM((n_col, BLK, snw), bf16),
            dma((n_row,)), dma((n_row,)), dma((n_col,)), dma((n_col,)),
            dma((n_row,)), dma((n_row,)), dma((n_pos,)), dma((n_pos,)),
            dma((n_pos,)), dma((n_pos,)), dma((n_pos,)), dma((n_pos,)), dma((4,)),
        ],
        compiler_params=pltpu.CompilerParams(
            collective_id=0, has_side_effects=True, vmem_limit_bytes=32 * 2**20
        ),
    )(perm, table, panel_raw.reshape(held, BLK, kw), diag_inverse)

    def row_spec(e):
        return pl.BlockSpec(
            (1, 1, BLK, snw),
            lambda i, t, p: (t[block_cols + 2 * i + e], (2 * i + e) // block_cols, 0, 0),
        )

    return pl.pallas_call(
        update_kernel,
        out_shape=jax.ShapeDtypeStruct(schur.shape, schur.dtype),
        grid_spec=pltpu.PrefetchScalarGridSpec(
            num_scalar_prefetch=2,
            grid=(block_rows // 2,),
            in_specs=[
                row_spec(0),
                row_spec(1),
                pl.BlockSpec((local_cols, snw), lambda i, t, p: (0, 0)),
                pl.BlockSpec((2 * BLK, local_cols), lambda i, t, p: (i, 0)),
            ],
            out_specs=pl.BlockSpec((2 * BLK, local_cols), lambda i, t, p: (i, 0)),
        ),
        compiler_params=pltpu.CompilerParams(vmem_limit_bytes=32 * 2**20),
    )(table, pattern, rows, rows, cols, schur)


def solution(mesh):
    return jax.shard_map(
        local,
        mesh=mesh,
        in_specs=(P("row", "col"), P("col", "row"), P(), P(), P("row", "col")),
        out_specs=P("row", "col"),
        check_vma=False,
    )
```

```python
import functools

import jax
import jax.numpy as jnp
from jax import lax
from jax.experimental import pallas as pl
from jax.experimental.pallas import tpu as pltpu
from jax.sharding import PartitionSpec as P

BLK = 128
MESH = pl.DeviceIdType.MESH


def times_inverse(left, right):
    return lax.dot_general(
        left, right, (((1,), (1,)), ((), ())), preferred_element_type=jnp.float32
    )


def exchange_kernel(
    n_row, n_col, gpr, held, block_cols,
    perm_ref, table_ref, raw_hbm, d_hbm, rows_ref, cols_ref,
    raw_ref, sorted_ref, a_ref, b_ref, own_ref, d_ref, cpan_ref,
    a_send, a_recv, b_send, b_recv, c_send, c_recv,
    up_send, up_recv, down_send, down_recv, f_send, f_recv, loc,
):
    r = lax.axis_index("row")
    c = lax.axis_index("col")
    n_pos = n_col // 2
    pos = c // 2
    core = c % 2
    sibling = pos * 2 + (1 - core)
    kw = raw_ref.shape[2]
    snw = d_ref.shape[0]
    load_raw = pltpu.make_async_copy(raw_hbm, raw_ref, loc.at[3])
    load_raw.start()
    load_d = pltpu.make_async_copy(d_hbm, d_ref, loc.at[0])
    load_d.start()

    def remote(src, dst, ssem, rsem, rr, cc):
        return pltpu.make_async_remote_copy(
            src_ref=src, dst_ref=dst, send_sem=ssem, recv_sem=rsem,
            device_id=(rr, cc), device_id_type=MESH,
        )

    def part(index):
        return pl.ds(pl.multiple_of(index * kw, kw), kw)

    barrier = pltpu.get_barrier_semaphore()
    for dr in range(1, n_row):
        pl.semaphore_signal(barrier, inc=1, device_id=((r + dr) % n_row, c), device_id_type=MESH)
    for dc in range(1, n_col):
        pl.semaphore_signal(barrier, inc=1, device_id=(r, (c + dc) % n_col), device_id_type=MESH)
    groups = [lax.div(perm_ref[c * held + i], block_cols) for i in range(held)]
    load_raw.wait()
    for g in range(n_col):
        block = 0
        for i in range(1, held):
            block = jnp.where(groups[i] == g, i, block)
        sorted_ref[g] = raw_ref[block]
    pl.semaphore_wait(barrier, n_row + n_col - 2)

    def a_copy(dr, came=None):
        to = (r + dr) % n_row
        return remote(sorted_ref.at[pl.ds(to * gpr, gpr)],
                      a_ref.at[:, :, part(r if came is None else came)],
                      a_send.at[dr], a_recv.at[dr], to, c)

    def b_copy(dc, came=None):
        to = (c + dc) % n_col
        return remote(sorted_ref.at[to], b_ref.at[c if came is None else came],
                      b_send.at[dc], b_recv.at[dc], r, to)

    for dr in range(1, n_row):
        a_copy(dr).start()
    for dc in range(1, n_col):
        b_copy(dc).start()
    a_ref[:, :, part(r)] = sorted_ref[pl.ds(r * gpr, gpr)]
    b_ref[c] = sorted_ref[c]
    load_d.wait()
    for dr in range(1, n_row):
        a_copy(dr, (r + n_row - dr) % n_row).wait_recv()
    def up_copy(d, q):
        slot = (pos - d) * 2 + core
        return remote(own_ref.at[q] if d == 0 else rows_ref.at[slot, q], rows_ref.at[slot, q],
                      up_send.at[d, q], up_recv.at[d, q], r, (pos + 1) * 2 + core)

    def down_copy(d, q):
        slot = (pos + d) * 2 + core
        return remote(own_ref.at[q] if d == 0 else rows_ref.at[slot, q], rows_ref.at[slot, q],
                      down_send.at[d, q], down_recv.at[d, q], r, (pos - 1) * 2 + core)

    def side_copy(source, q, mine):
        slot = source * 2 + core
        return remote(own_ref.at[q] if mine else rows_ref.at[slot, q], rows_ref.at[slot, q],
                      f_send.at[source, q], f_recv.at[source, q], r, sibling)

    for q in range(gpr):
        own_ref[q] = times_inverse(a_ref[q], d_ref[...]).astype(jnp.bfloat16)

        @pl.when(pos < n_pos - 1)
        def _(q=q):
            up_copy(0, q).start()

        @pl.when(pos > 0)
        def _(q=q):
            down_copy(0, q).start()

    for q in range(gpr):
        side_copy(pos, q, True).start()
    keep = pltpu.make_async_copy(own_ref, rows_ref.at[c], loc.at[1])
    keep.start()

    for dc in range(1, n_col):
        b_copy(dc, (c + n_col - dc) % n_col).wait_recv()

    def c_copy(dr, came=None):
        return remote(b_ref, cpan_ref.at[:, :, part(r if came is None else came)],
                      c_send.at[dr], c_recv.at[dr], (r + dr) % n_row, c)

    for dr in range(1, n_row):
        c_copy(dr).start()
    cpan_ref[:, :, part(r)] = b_ref[...]

    def factor_columns():
        for dr in range(1, n_row):
            c_copy(dr, (r + n_row - dr) % n_row).wait_recv()
        step = 4 if block_cols % 4 == 0 else 1
        for w in range(0, block_cols, step):
            left = jnp.concatenate([cpan_ref[table_ref[w + k]] for k in range(step)], axis=0)
            done = times_inverse(left, d_ref[...]).astype(jnp.bfloat16)
            cols_ref[w * BLK:(w + step) * BLK, :] = done

    for d in range(1, n_pos):
        if d == n_pos - 1:
            factor_columns()

        for q in range(gpr):
            @pl.when(pos - d >= 0)
            def _(d=d, q=q):
                slot = (pos - d) * 2 + core
                remote(own_ref.at[q], rows_ref.at[slot, q], up_send.at[d - 1, q],
                       up_recv.at[d - 1, q], r, sibling).wait_recv()
                if d < n_pos - 1:
                    @pl.when(pos < n_pos - 1)
                    def _():
                        up_copy(d, q).start()
                side_copy(pos - d, q, False).start()

            @pl.when(pos + d <= n_pos - 1)
            def _(d=d, q=q):
                slot = (pos + d) * 2 + core
                remote(own_ref.at[q], rows_ref.at[slot, q], down_send.at[d - 1, q],
                       down_recv.at[d - 1, q], r, sibling).wait_recv()
                if d < n_pos - 1:
                    @pl.when(pos > 0)
                    def _():
                        down_copy(d, q).start()
                side_copy(pos + d, q, False).start()

    for dr in range(1, n_row):
        a_copy(dr).wait_send()
        c_copy(dr).wait_send()
    for dc in range(1, n_col):
        b_copy(dc).wait_send()
    for q in range(gpr):
        for d in range(n_pos - 1):
            @pl.when((pos - d >= 0) & (pos < n_pos - 1))
            def _(d=d, q=q):
                up_copy(d, q).wait_send()

            @pl.when((pos + d <= n_pos - 1) & (pos > 0))
            def _(d=d, q=q):
                down_copy(d, q).wait_send()
        for source in range(n_pos):
            slot = source * 2 + (1 - core)
            remote(own_ref.at[q], rows_ref.at[slot, q], f_send.at[source, q],
                   f_recv.at[source, q], r, sibling).wait_recv()
            side_copy(source, q, True).wait_send()
    keep.wait()


def update_kernel(
    table, pat_ref, low_ref, high_ref, cols_ref, schur_ref, out_ref,
):
    i = pl.program_id(0)
    left = jnp.concatenate([low_ref[0, 0], high_ref[0, 0]], axis=0)
    update = times_inverse(left, cols_ref[...])
    for e in range(2):
        rows = slice(e * BLK, (e + 1) * BLK)
        for w in range(cols_ref.shape[0] // BLK):
            at = slice(w * BLK, (w + 1) * BLK)
            weight = pat_ref[2 * i + e, w].astype(jnp.float32)
            out_ref[rows, at] = schur_ref[rows, at] - update[rows, at] * weight


def local(schur, panel_raw, diag_inverse, perm, pattern):
    n_row = lax.axis_size("row")
    n_col = lax.axis_size("col")
    r = lax.axis_index("row")
    c = lax.axis_index("col")
    local_rows, local_cols = schur.shape
    block_rows, block_cols = local_rows // BLK, local_cols // BLK
    gpr = local_rows // local_cols
    held, kw = panel_raw.shape[0] // BLK, panel_raw.shape[1]
    snw = diag_inverse.shape[0]
    blocks = perm.shape[0]
    bf16 = jnp.bfloat16

    at = jnp.arange(block_cols + block_rows, dtype=jnp.int32)
    ids = jnp.where(at < block_cols, c * block_cols + at, r * block_rows + at - block_cols)
    holder = lax.div(lax.broadcasted_iota(jnp.int32, (ids.shape[0], blocks), 1), held)
    table = jnp.sum(jnp.where(perm[None, :] == ids[:, None], holder, 0), axis=1)
    n_pos = n_col // 2
    dma = pltpu.SemaphoreType.DMA
    smem = pl.BlockSpec(memory_space=pltpu.SMEM)
    hbm = pl.BlockSpec(memory_space=pltpu.HBM)
    rows, cols = pl.pallas_call(
        functools.partial(exchange_kernel, n_row, n_col, gpr, held, block_cols),
        out_shape=(
            jax.ShapeDtypeStruct((n_col, gpr, BLK, snw), bf16),
            jax.ShapeDtypeStruct((local_cols, snw), bf16),
        ),
        in_specs=[smem, smem, hbm, hbm],
        out_specs=(
            pl.BlockSpec(memory_space=pl.ANY),
            pl.BlockSpec(memory_space=pltpu.VMEM),
        ),
        scratch_shapes=[
            pltpu.VMEM((held, BLK, kw), bf16),
            pltpu.VMEM((n_col, BLK, kw), bf16),
            pltpu.VMEM((gpr, BLK, snw), bf16),
            pltpu.VMEM((n_col, BLK, kw), bf16),
            pltpu.VMEM((gpr, BLK, snw), bf16),
            pltpu.VMEM((snw, snw), bf16),
            pltpu.VMEM((n_col, BLK, snw), bf16),
            dma((n_row,)), dma((n_row,)), dma((n_col,)), dma((n_col,)),
            dma((n_row,)), dma((n_row,)), dma((n_pos, gpr)), dma((n_pos, gpr)),
            dma((n_pos, gpr)), dma((n_pos, gpr)), dma((n_pos, gpr)), dma((n_pos, gpr)), dma((4,)),
        ],
        compiler_params=pltpu.CompilerParams(
            collective_id=0, has_side_effects=True, vmem_limit_bytes=20 * 2**20
        ),
        cost_estimate=pl.CostEstimate(
            flops=2 * (local_cols + gpr * BLK) * snw * snw,
            bytes_accessed=30 * local_rows * snw,
            transcendentals=0,
        ),
    )(perm, table, panel_raw.reshape(held, BLK, kw), diag_inverse)

    def row_spec(e):
        return pl.BlockSpec(
            (1, 1, BLK, snw),
            lambda i, t, p: (t[block_cols + 2 * i + e], (2 * i + e) // block_cols, 0, 0),
        )

    return pl.pallas_call(
        update_kernel,
        out_shape=jax.ShapeDtypeStruct(schur.shape, schur.dtype),
        grid_spec=pltpu.PrefetchScalarGridSpec(
            num_scalar_prefetch=2,
            grid=(block_rows // 2,),
            in_specs=[
                row_spec(0),
                row_spec(1),
                pl.BlockSpec((local_cols, snw), lambda i, t, p: (0, 0)),
                pl.BlockSpec((2 * BLK, local_cols), lambda i, t, p: (i, 0)),
            ],
            out_specs=pl.BlockSpec((2 * BLK, local_cols), lambda i, t, p: (i, 0)),
        ),
        compiler_params=pltpu.CompilerParams(vmem_limit_bytes=20 * 2**20),
    )(table, pattern, rows, rows, cols, schur)


def solution(mesh):
    return jax.shard_map(
        local,
        mesh=mesh,
        in_specs=(P("row", "col"), P("col", "row"), P(), P(), P("row", "col")),
        out_specs=P("row", "col"),
        check_vma=False,
    )
```

```python
import functools

import jax
import jax.numpy as jnp
from jax import lax
from jax.experimental import pallas as pl
from jax.experimental.pallas import tpu as pltpu
from jax.sharding import PartitionSpec as P

BLK = 128
MESH = pl.DeviceIdType.MESH


def times_inverse(left, right):
    return lax.dot_general(
        left, right, (((1,), (1,)), ((), ())), preferred_element_type=jnp.float32
    )


def exchange_kernel(
    n_row, n_col, gpr, held, block_cols, block_rows,
    perm_ref, raw_hbm, d_hbm, rows_ref, cols_ref, table_ref,
    raw_ref, sorted_ref, a_ref, b_ref, own_ref, d_ref, cpan_ref,
    a_send, a_recv, b_send, b_recv, c_send, c_recv,
    up_send, up_recv, down_send, down_recv, f_send, f_recv, loc,
):
    r = lax.axis_index("row")
    c = lax.axis_index("col")
    n_pos = n_col // 2
    pos = c // 2
    core = c % 2
    sibling = pos * 2 + (1 - core)
    kw = raw_ref.shape[2]
    snw = d_ref.shape[0]
    load_raw = pltpu.make_async_copy(raw_hbm, raw_ref, loc.at[3])
    load_raw.start()
    load_d = pltpu.make_async_copy(d_hbm, d_ref, loc.at[0])
    load_d.start()

    def remote(src, dst, ssem, rsem, rr, cc):
        return pltpu.make_async_remote_copy(
            src_ref=src, dst_ref=dst, send_sem=ssem, recv_sem=rsem,
            device_id=(rr, cc), device_id_type=MESH,
        )

    def part(index):
        return pl.ds(pl.multiple_of(index * kw, kw), kw)

    barrier = pltpu.get_barrier_semaphore()
    for dr in range(1, n_row):
        pl.semaphore_signal(barrier, inc=1, device_id=((r + dr) % n_row, c), device_id_type=MESH)
    for dc in range(1, n_col):
        pl.semaphore_signal(barrier, inc=1, device_id=(r, (c + dc) % n_col), device_id_type=MESH)
    groups = [lax.div(perm_ref[c * held + i], block_cols) for i in range(held)]
    load_raw.wait()
    for g in range(n_col):
        block = 0
        for i in range(1, held):
            block = jnp.where(groups[i] == g, i, block)
        sorted_ref[g] = raw_ref[block]
    pl.semaphore_wait(barrier, n_row + n_col - 2)

    def a_copy(dr, came=None):
        to = (r + dr) % n_row
        return remote(sorted_ref.at[pl.ds(to * gpr, gpr)],
                      a_ref.at[:, :, part(r if came is None else came)],
                      a_send.at[dr], a_recv.at[dr], to, c)

    def b_copy(dc, came=None):
        to = (c + dc) % n_col
        return remote(sorted_ref.at[to], b_ref.at[c if came is None else came],
                      b_send.at[dc], b_recv.at[dc], r, to)

    for dr in range(1, n_row):
        a_copy(dr).start()
    for dc in range(1, n_col):
        b_copy(dc).start()
    a_ref[:, :, part(r)] = sorted_ref[pl.ds(r * gpr, gpr)]
    b_ref[c] = sorted_ref[c]
    load_d.wait()
    for dr in range(1, n_row):
        a_copy(dr, (r + n_row - dr) % n_row).wait_recv()
    def up_copy(d, q):
        slot = (pos - d) * 2 + core
        return remote(own_ref.at[q] if d == 0 else rows_ref.at[slot, q], rows_ref.at[slot, q],
                      up_send.at[d, q], up_recv.at[d, q], r, (pos + 1) * 2 + core)

    def down_copy(d, q):
        slot = (pos + d) * 2 + core
        return remote(own_ref.at[q] if d == 0 else rows_ref.at[slot, q], rows_ref.at[slot, q],
                      down_send.at[d, q], down_recv.at[d, q], r, (pos - 1) * 2 + core)

    def side_copy(source, q, mine):
        slot = source * 2 + core
        return remote(own_ref.at[q] if mine else rows_ref.at[slot, q], rows_ref.at[slot, q],
                      f_send.at[source, q], f_recv.at[source, q], r, sibling)

    for q in range(gpr):
        own_ref[q] = times_inverse(a_ref[q], d_ref[...]).astype(jnp.bfloat16)

        @pl.when(pos < n_pos - 1)
        def _(q=q):
            up_copy(0, q).start()

        @pl.when(pos > 0)
        def _(q=q):
            down_copy(0, q).start()

    for q in range(gpr):
        side_copy(pos, q, True).start()
    keep = pltpu.make_async_copy(own_ref, rows_ref.at[c], loc.at[1])
    keep.start()

    for dc in range(1, n_col):
        b_copy(dc, (c + n_col - dc) % n_col).wait_recv()

    def c_copy(dr, came=None):
        return remote(b_ref, cpan_ref.at[:, :, part(r if came is None else came)],
                      c_send.at[dr], c_recv.at[dr], (r + dr) % n_row, c)

    for dr in range(1, n_row):
        c_copy(dr).start()
    cpan_ref[:, :, part(r)] = b_ref[...]

    wanted = [c * block_cols + k for k in range(block_cols)]
    wanted += [r * block_rows + k for k in range(block_rows)]

    def look(p, found):
        at, holder = perm_ref[p], p // held
        return tuple(jnp.where(at == w, holder, f) for w, f in zip(wanted, found))

    holders = lax.fori_loop(
        0, perm_ref.shape[0], look, tuple(jnp.int32(0) for _ in wanted)
    )
    for k, value in enumerate(holders):
        table_ref[k] = value

    def factor_columns():
        for dr in range(1, n_row):
            c_copy(dr, (r + n_row - dr) % n_row).wait_recv()
        step = 4 if block_cols % 4 == 0 else 1
        for w in range(0, block_cols, step):
            left = jnp.concatenate([cpan_ref[holders[w + k]] for k in range(step)], axis=0)
            done = times_inverse(left, d_ref[...]).astype(jnp.bfloat16)
            cols_ref[w * BLK:(w + step) * BLK, :] = done

    for d in range(1, n_pos):
        if d == n_pos - 1:
            factor_columns()

        for q in range(gpr):
            @pl.when(pos - d >= 0)
            def _(d=d, q=q):
                slot = (pos - d) * 2 + core
                remote(own_ref.at[q], rows_ref.at[slot, q], up_send.at[d - 1, q],
                       up_recv.at[d - 1, q], r, sibling).wait_recv()
                if d < n_pos - 1:
                    @pl.when(pos < n_pos - 1)
                    def _():
                        up_copy(d, q).start()
                side_copy(pos - d, q, False).start()

            @pl.when(pos + d <= n_pos - 1)
            def _(d=d, q=q):
                slot = (pos + d) * 2 + core
                remote(own_ref.at[q], rows_ref.at[slot, q], down_send.at[d - 1, q],
                       down_recv.at[d - 1, q], r, sibling).wait_recv()
                if d < n_pos - 1:
                    @pl.when(pos > 0)
                    def _():
                        down_copy(d, q).start()
                side_copy(pos + d, q, False).start()

    for dr in range(1, n_row):
        a_copy(dr).wait_send()
        c_copy(dr).wait_send()
    for dc in range(1, n_col):
        b_copy(dc).wait_send()
    for q in range(gpr):
        for d in range(n_pos - 1):
            @pl.when((pos - d >= 0) & (pos < n_pos - 1))
            def _(d=d, q=q):
                up_copy(d, q).wait_send()

            @pl.when((pos + d <= n_pos - 1) & (pos > 0))
            def _(d=d, q=q):
                down_copy(d, q).wait_send()
        for source in range(n_pos):
            slot = source * 2 + (1 - core)
            remote(own_ref.at[q], rows_ref.at[slot, q], f_send.at[source, q],
                   f_recv.at[source, q], r, sibling).wait_recv()
            side_copy(source, q, True).wait_send()
    keep.wait()


def update_kernel(tile, table, pat_ref, *refs):
    row_refs, (cols_ref, schur_ref, out_ref) = refs[:tile], refs[tile:]
    i = pl.program_id(0)
    left = jnp.concatenate([ref[0, 0] for ref in row_refs], axis=0)
    update = times_inverse(left, cols_ref[...])
    for e in range(tile):
        rows = slice(e * BLK, (e + 1) * BLK)
        for w in range(cols_ref.shape[0] // BLK):
            at = slice(w * BLK, (w + 1) * BLK)
            weight = pat_ref[w, tile * i + e].astype(jnp.float32)
            out_ref[rows, at] = schur_ref[rows, at] - update[rows, at] * weight


def local(schur, panel_raw, diag_inverse, perm, pattern):
    n_row = lax.axis_size("row")
    n_col = lax.axis_size("col")
    r = lax.axis_index("row")
    c = lax.axis_index("col")
    local_rows, local_cols = schur.shape
    block_rows, block_cols = local_rows // BLK, local_cols // BLK
    gpr = local_rows // local_cols
    held, kw = panel_raw.shape[0] // BLK, panel_raw.shape[1]
    snw = diag_inverse.shape[0]
    blocks = perm.shape[0]
    bf16 = jnp.bfloat16

    n_pos = n_col // 2
    dma = pltpu.SemaphoreType.DMA
    smem = pl.BlockSpec(memory_space=pltpu.SMEM)
    hbm = pl.BlockSpec(memory_space=pltpu.HBM)
    rows, cols, table = pl.pallas_call(
        functools.partial(exchange_kernel, n_row, n_col, gpr, held, block_cols, block_rows),
        out_shape=(
            jax.ShapeDtypeStruct((n_col, gpr, BLK, snw), bf16),
            jax.ShapeDtypeStruct((local_cols, snw), bf16),
            jax.ShapeDtypeStruct((block_cols + block_rows,), jnp.int32),
        ),
        in_specs=[smem, hbm, hbm],
        out_specs=(
            pl.BlockSpec(memory_space=pl.ANY),
            pl.BlockSpec(memory_space=pltpu.VMEM),
            smem,
        ),
        scratch_shapes=[
            pltpu.VMEM((held, BLK, kw), bf16),
            pltpu.VMEM((n_col, BLK, kw), bf16),
            pltpu.VMEM((gpr, BLK, snw), bf16),
            pltpu.VMEM((n_col, BLK, kw), bf16),
            pltpu.VMEM((gpr, BLK, snw), bf16),
            pltpu.VMEM((snw, snw), bf16),
            pltpu.VMEM((n_col, BLK, snw), bf16),
            dma((n_row,)), dma((n_row,)), dma((n_col,)), dma((n_col,)),
            dma((n_row,)), dma((n_row,)), dma((n_pos, gpr)), dma((n_pos, gpr)),
            dma((n_pos, gpr)), dma((n_pos, gpr)), dma((n_pos, gpr)), dma((n_pos, gpr)), dma((4,)),
        ],
        compiler_params=pltpu.CompilerParams(
            collective_id=0, has_side_effects=True, vmem_limit_bytes=20 * 2**20
        ),
        cost_estimate=pl.CostEstimate(
            flops=2 * (local_cols + gpr * BLK) * snw * snw,
            bytes_accessed=30 * local_rows * snw,
            transcendentals=0,
        ),
    )(perm, panel_raw.reshape(held, BLK, kw), diag_inverse)

    tile = 4 if block_rows % 4 == 0 else 1

    def row_spec(e):
        return pl.BlockSpec(
            (1, 1, BLK, snw),
            lambda i, t, p: (t[block_cols + tile * i + e], (tile * i + e) // block_cols, 0, 0),
        )

    wide = pl.BlockSpec((tile * BLK, local_cols), lambda i, t, p: (i, 0))
    return pl.pallas_call(
        functools.partial(update_kernel, tile),
        out_shape=jax.ShapeDtypeStruct(schur.shape, schur.dtype),
        grid_spec=pltpu.PrefetchScalarGridSpec(
            num_scalar_prefetch=2,
            grid=(block_rows // tile,),
            in_specs=[row_spec(e) for e in range(tile)]
            + [pl.BlockSpec((local_cols, snw), lambda i, t, p: (0, 0)), wide],
            out_specs=wide,
        ),
        compiler_params=pltpu.CompilerParams(vmem_limit_bytes=28 * 2**20),
    )(table, pattern.T, *([rows] * tile), cols, schur)


def solution(mesh):
    return jax.shard_map(
        local,
        mesh=mesh,
        in_specs=(P("row", "col"), P("col", "row"), P(), P(), P("row", "col")),
        out_specs=P("row", "col"),
        check_vma=False,
    )
```

```python
import functools

import jax
import jax.numpy as jnp
from jax import lax
from jax.experimental import pallas as pl
from jax.experimental.pallas import tpu as pltpu
from jax.sharding import PartitionSpec as P

BLK = 128
MESH = pl.DeviceIdType.MESH


def times_inverse(left, right):
    return lax.dot_general(
        left, right, (((1,), (1,)), ((), ())), preferred_element_type=jnp.float32
    )


def exchange_kernel(
    n_row, n_col, gpr, held, block_cols, block_rows,
    perm_ref, raw_hbm, d_hbm, rows_ref, cols_hbm, table_ref,
    raw_ref, sorted_ref, a_ref, b_ref, own_ref, d_ref, cpan_ref, cols_ref,
    a_send, a_recv, b_send, b_recv, c_send, c_recv,
    up_send, up_recv, down_send, down_recv, f_send, f_recv, loc,
):
    r = lax.axis_index("row")
    c = lax.axis_index("col")
    n_pos = n_col // 2
    pos = c // 2
    core = c % 2
    sibling = pos * 2 + (1 - core)
    kw = raw_ref.shape[2]
    snw = d_ref.shape[0]
    load_raw = pltpu.make_async_copy(raw_hbm, raw_ref, loc.at[3])
    load_raw.start()
    load_d = pltpu.make_async_copy(d_hbm, d_ref, loc.at[0])
    load_d.start()

    def remote(src, dst, ssem, rsem, rr, cc):
        return pltpu.make_async_remote_copy(
            src_ref=src, dst_ref=dst, send_sem=ssem, recv_sem=rsem,
            device_id=(rr, cc), device_id_type=MESH,
        )

    def part(index):
        return pl.ds(pl.multiple_of(index * kw, kw), kw)

    barrier = pltpu.get_barrier_semaphore()
    for dr in range(1, n_row):
        pl.semaphore_signal(barrier, inc=1, device_id=((r + dr) % n_row, c), device_id_type=MESH)
    for dc in range(1, n_col):
        pl.semaphore_signal(barrier, inc=1, device_id=(r, (c + dc) % n_col), device_id_type=MESH)
    groups = [lax.div(perm_ref[c * held + i], block_cols) for i in range(held)]
    load_raw.wait()
    for g in range(n_col):
        block = 0
        for i in range(1, held):
            block = jnp.where(groups[i] == g, i, block)
        sorted_ref[g] = raw_ref[block]
    pl.semaphore_wait(barrier, n_row + n_col - 2)

    def a_copy(dr, q, came=None):
        to = (r + dr) % n_row
        return remote(sorted_ref.at[to * gpr + q],
                      a_ref.at[q, :, part(r if came is None else came)],
                      a_send.at[dr, q], a_recv.at[dr, q], to, c)

    def b_copy(dc, came=None):
        to = (c + dc) % n_col
        return remote(sorted_ref.at[to], b_ref.at[c if came is None else came],
                      b_send.at[dc], b_recv.at[dc], r, to)

    for q in range(gpr):
        for dr in range(1, n_row):
            a_copy(dr, q).start()
    for dc in range(1, n_col):
        b_copy(dc).start()
    a_ref[:, :, part(r)] = sorted_ref[pl.ds(r * gpr, gpr)]
    b_ref[c] = sorted_ref[c]
    load_d.wait()
    def up_copy(d, q):
        slot = (pos - d) * 2 + core
        return remote(own_ref.at[q] if d == 0 else rows_ref.at[slot, q], rows_ref.at[slot, q],
                      up_send.at[d, q], up_recv.at[d, q], r, (pos + 1) * 2 + core)

    def down_copy(d, q):
        slot = (pos + d) * 2 + core
        return remote(own_ref.at[q] if d == 0 else rows_ref.at[slot, q], rows_ref.at[slot, q],
                      down_send.at[d, q], down_recv.at[d, q], r, (pos - 1) * 2 + core)

    def side_copy(source, q, mine):
        slot = source * 2 + core
        return remote(own_ref.at[q] if mine else rows_ref.at[slot, q], rows_ref.at[slot, q],
                      f_send.at[source, q], f_recv.at[source, q], r, sibling)

    for q in range(gpr):
        for dr in range(1, n_row):
            a_copy(dr, q, (r + n_row - dr) % n_row).wait_recv()
        own_ref[q] = times_inverse(a_ref[q], d_ref[...]).astype(jnp.bfloat16)

        @pl.when(pos < n_pos - 1)
        def _(q=q):
            up_copy(0, q).start()

        @pl.when(pos > 0)
        def _(q=q):
            down_copy(0, q).start()

    for q in range(gpr):
        side_copy(pos, q, True).start()
    keep = pltpu.make_async_copy(own_ref, rows_ref.at[c], loc.at[1])
    keep.start()

    for dc in range(1, n_col):
        b_copy(dc, (c + n_col - dc) % n_col).wait_recv()

    def c_copy(dr, came=None):
        return remote(b_ref, cpan_ref.at[:, :, part(r if came is None else came)],
                      c_send.at[dr], c_recv.at[dr], (r + dr) % n_row, c)

    for dr in range(1, n_row):
        c_copy(dr).start()
    cpan_ref[:, :, part(r)] = b_ref[...]

    wanted = [c * block_cols + k for k in range(block_cols)]
    wanted += [r * block_rows + k for k in range(block_rows)]

    def look(p, found):
        at, holder = perm_ref[p], p // held
        return tuple(jnp.where(at == w, holder, f) for w, f in zip(wanted, found))

    holders = lax.fori_loop(
        0, perm_ref.shape[0], look, tuple(jnp.int32(0) for _ in wanted)
    )
    for k, value in enumerate(holders):
        table_ref[k] = value

    keep_cols = pltpu.make_async_copy(cols_ref, cols_hbm, loc.at[2])

    def factor_columns():
        for dr in range(1, n_row):
            c_copy(dr, (r + n_row - dr) % n_row).wait_recv()
        step = 4 if block_cols % 4 == 0 else 1
        for w in range(0, block_cols, step):
            left = jnp.concatenate([cpan_ref[holders[w + k]] for k in range(step)], axis=0)
            done = times_inverse(left, d_ref[...]).astype(jnp.bfloat16)
            cols_ref[w * BLK:(w + step) * BLK, :] = done
        keep_cols.start()

    for d in range(1, n_pos):
        if d == n_pos - 1:
            factor_columns()

        for q in range(gpr):
            @pl.when(pos - d >= 0)
            def _(d=d, q=q):
                slot = (pos - d) * 2 + core
                remote(own_ref.at[q], rows_ref.at[slot, q], up_send.at[d - 1, q],
                       up_recv.at[d - 1, q], r, sibling).wait_recv()
                if d < n_pos - 1:
                    @pl.when(pos < n_pos - 1)
                    def _():
                        up_copy(d, q).start()
                side_copy(pos - d, q, False).start()

            @pl.when(pos + d <= n_pos - 1)
            def _(d=d, q=q):
                slot = (pos + d) * 2 + core
                remote(own_ref.at[q], rows_ref.at[slot, q], down_send.at[d - 1, q],
                       down_recv.at[d - 1, q], r, sibling).wait_recv()
                if d < n_pos - 1:
                    @pl.when(pos > 0)
                    def _():
                        down_copy(d, q).start()
                side_copy(pos + d, q, False).start()

    for dr in range(1, n_row):
        for q in range(gpr):
            a_copy(dr, q).wait_send()
        c_copy(dr).wait_send()
    for dc in range(1, n_col):
        b_copy(dc).wait_send()
    for q in range(gpr):
        for d in range(n_pos - 1):
            @pl.when((pos - d >= 0) & (pos < n_pos - 1))
            def _(d=d, q=q):
                up_copy(d, q).wait_send()

            @pl.when((pos + d <= n_pos - 1) & (pos > 0))
            def _(d=d, q=q):
                down_copy(d, q).wait_send()
        for source in range(n_pos):
            slot = source * 2 + (1 - core)
            remote(own_ref.at[q], rows_ref.at[slot, q], f_send.at[source, q],
                   f_recv.at[source, q], r, sibling).wait_recv()
            side_copy(source, q, True).wait_send()
    keep.wait()
    keep_cols.wait()


def update_kernel(tile, table, pat_ref, *refs):
    row_refs, (cols_ref, schur_ref, out_ref) = refs[:tile], refs[tile:]
    i = pl.program_id(0)
    left = jnp.concatenate([ref[0, 0] for ref in row_refs], axis=0)
    update = times_inverse(left, cols_ref[...])
    for e in range(tile):
        rows = slice(e * BLK, (e + 1) * BLK)
        for w in range(cols_ref.shape[0] // BLK):
            at = slice(w * BLK, (w + 1) * BLK)
            weight = pat_ref[w, tile * i + e].astype(jnp.float32)
            out_ref[rows, at] = schur_ref[rows, at] - update[rows, at] * weight


def local(schur, panel_raw, diag_inverse, perm, pattern):
    n_row = lax.axis_size("row")
    n_col = lax.axis_size("col")
    r = lax.axis_index("row")
    c = lax.axis_index("col")
    local_rows, local_cols = schur.shape
    block_rows, block_cols = local_rows // BLK, local_cols // BLK
    gpr = local_rows // local_cols
    held, kw = panel_raw.shape[0] // BLK, panel_raw.shape[1]
    snw = diag_inverse.shape[0]
    blocks = perm.shape[0]
    bf16 = jnp.bfloat16

    n_pos = n_col // 2
    dma = pltpu.SemaphoreType.DMA
    smem = pl.BlockSpec(memory_space=pltpu.SMEM)
    hbm = pl.BlockSpec(memory_space=pltpu.HBM)
    rows, cols, table = pl.pallas_call(
        functools.partial(exchange_kernel, n_row, n_col, gpr, held, block_cols, block_rows),
        out_shape=(
            jax.ShapeDtypeStruct((n_col, gpr, BLK, snw), bf16),
            jax.ShapeDtypeStruct((local_cols, snw), bf16),
            jax.ShapeDtypeStruct((block_cols + block_rows,), jnp.int32),
        ),
        in_specs=[smem, hbm, hbm],
        out_specs=(
            pl.BlockSpec(memory_space=pl.ANY),
            pl.BlockSpec(memory_space=pl.ANY),
            smem,
        ),
        scratch_shapes=[
            pltpu.VMEM((held, BLK, kw), bf16),
            pltpu.VMEM((n_col, BLK, kw), bf16),
            pltpu.VMEM((gpr, BLK, snw), bf16),
            pltpu.VMEM((n_col, BLK, kw), bf16),
            pltpu.VMEM((gpr, BLK, snw), bf16),
            pltpu.VMEM((snw, snw), bf16),
            pltpu.VMEM((n_col, BLK, snw), bf16),
            pltpu.VMEM((local_cols, snw), bf16),
            dma((n_row, gpr)), dma((n_row, gpr)), dma((n_col,)), dma((n_col,)),
            dma((n_row,)), dma((n_row,)), dma((n_pos, gpr)), dma((n_pos, gpr)),
            dma((n_pos, gpr)), dma((n_pos, gpr)), dma((n_pos, gpr)), dma((n_pos, gpr)), dma((4,)),
        ],
        compiler_params=pltpu.CompilerParams(
            collective_id=0, has_side_effects=True, vmem_limit_bytes=58 * 2**20
        ),
        cost_estimate=pl.CostEstimate(
            flops=2 * (local_cols + gpr * BLK) * snw * snw,
            bytes_accessed=30 * local_rows * snw,
            transcendentals=0,
        ),
    )(perm, panel_raw.reshape(held, BLK, kw), diag_inverse)

    tile = 4 if block_rows % 4 == 0 else 1

    def row_spec(e):
        return pl.BlockSpec(
            (1, 1, BLK, snw),
            lambda i, t, p: (t[block_cols + tile * i + e], (tile * i + e) // block_cols, 0, 0),
        )

    wide = pl.BlockSpec((tile * BLK, local_cols), lambda i, t, p: (i, 0))
    return pl.pallas_call(
        functools.partial(update_kernel, tile),
        out_shape=jax.ShapeDtypeStruct(schur.shape, schur.dtype),
        grid_spec=pltpu.PrefetchScalarGridSpec(
            num_scalar_prefetch=2,
            grid=(block_rows // tile,),
            in_specs=[row_spec(e) for e in range(tile)]
            + [pl.BlockSpec((local_cols, snw), lambda i, t, p: (0, 0)), wide],
            out_specs=wide,
        ),
        compiler_params=pltpu.CompilerParams(vmem_limit_bytes=58 * 2**20),
    )(table, pattern.T, *([rows] * tile), cols, schur)


def solution(mesh):
    return jax.shard_map(
        local,
        mesh=mesh,
        in_specs=(P("row", "col"), P("col", "row"), P(), P(), P("row", "col")),
        out_specs=P("row", "col"),
        check_vma=False,
    )
```

```python
import functools

import jax
import jax.numpy as jnp
from jax import lax
from jax.experimental import pallas as pl
from jax.experimental.pallas import tpu as pltpu
from jax.sharding import PartitionSpec as P

BLK = 128
MESH = pl.DeviceIdType.MESH


def times_inverse(left, right):
    return lax.dot_general(
        left, right, (((1,), (1,)), ((), ())), preferred_element_type=jnp.float32
    )


def exchange_kernel(
    n_row, n_col, gpr, held, block_cols, block_rows,
    perm_ref, raw_hbm, d_hbm, rows_ref, cols_hbm, table_ref,
    raw_ref, sorted_ref, a_ref, b_ref, own_ref, d_ref, cpan_ref, cols_ref,
    a_send, a_recv, b_send, b_recv, c_send, c_recv,
    up_send, up_recv, down_send, down_recv, f_send, f_recv, loc,
):
    r = lax.axis_index("row")
    c = lax.axis_index("col")
    n_pos = n_col // 2
    pos = c // 2
    core = c % 2
    sibling = pos * 2 + (1 - core)
    kw = raw_ref.shape[2]
    snw = d_ref.shape[0]
    load_raw = pltpu.make_async_copy(raw_hbm, raw_ref, loc.at[3])
    load_raw.start()
    load_d = pltpu.make_async_copy(d_hbm, d_ref, loc.at[0])
    load_d.start()

    def remote(src, dst, ssem, rsem, rr, cc):
        return pltpu.make_async_remote_copy(
            src_ref=src, dst_ref=dst, send_sem=ssem, recv_sem=rsem,
            device_id=(rr, cc), device_id_type=MESH,
        )

    def part(index):
        return pl.ds(pl.multiple_of(index * kw, kw), kw)

    barrier = pltpu.get_barrier_semaphore()
    for dr in range(1, n_row):
        pl.semaphore_signal(barrier, inc=1, device_id=((r + dr) % n_row, c), device_id_type=MESH)
    for dc in range(1, n_col):
        pl.semaphore_signal(barrier, inc=1, device_id=(r, (c + dc) % n_col), device_id_type=MESH)
    groups = [lax.div(perm_ref[c * held + i], block_cols) for i in range(held)]
    load_raw.wait()
    for g in range(n_col):
        block = 0
        for i in range(1, held):
            block = jnp.where(groups[i] == g, i, block)
        sorted_ref[g] = raw_ref[block]
    pl.semaphore_wait(barrier, n_row + n_col - 2)

    def a_copy(dr, q, came=None):
        to = (r + dr) % n_row
        return remote(sorted_ref.at[to * gpr + q],
                      a_ref.at[q, :, part(r if came is None else came)],
                      a_send.at[dr, q], a_recv.at[dr, q], to, c)

    def b_copy(dc, came=None):
        to = (c + dc) % n_col
        return remote(sorted_ref.at[to], b_ref.at[c if came is None else came],
                      b_send.at[dc], b_recv.at[dc], r, to)

    for q in range(gpr):
        for dr in range(1, n_row):
            a_copy(dr, q).start()
    for dc in range(1, n_col):
        b_copy(dc).start()
    a_ref[:, :, part(r)] = sorted_ref[pl.ds(r * gpr, gpr)]
    b_ref[c] = sorted_ref[c]
    load_d.wait()
    def up_copy(d, q):
        slot = (pos - d) * 2 + core
        return remote(own_ref.at[q] if d == 0 else rows_ref.at[slot, q], rows_ref.at[slot, q],
                      up_send.at[d, q], up_recv.at[d, q], r, (pos + 1) * 2 + core)

    def down_copy(d, q):
        slot = (pos + d) * 2 + core
        return remote(own_ref.at[q] if d == 0 else rows_ref.at[slot, q], rows_ref.at[slot, q],
                      down_send.at[d, q], down_recv.at[d, q], r, (pos - 1) * 2 + core)

    def side_copy(source, q, mine):
        slot = source * 2 + core
        return remote(own_ref.at[q] if mine else rows_ref.at[slot, q], rows_ref.at[slot, q],
                      f_send.at[source, q], f_recv.at[source, q], r, sibling)

    for q in range(gpr):
        for dr in range(1, n_row):
            a_copy(dr, q, (r + n_row - dr) % n_row).wait_recv()
        own_ref[q] = times_inverse(a_ref[q], d_ref[...]).astype(jnp.bfloat16)

        @pl.when(pos < n_pos - 1)
        def _(q=q):
            up_copy(0, q).start()

        @pl.when(pos > 0)
        def _(q=q):
            down_copy(0, q).start()

    for q in range(gpr):
        side_copy(pos, q, True).start()
    keep = pltpu.make_async_copy(own_ref, rows_ref.at[c], loc.at[1])
    keep.start()

    for dc in range(1, n_col):
        b_copy(dc, (c + n_col - dc) % n_col).wait_recv()

    def c_copy(dr, came=None):
        return remote(b_ref, cpan_ref.at[:, :, part(r if came is None else came)],
                      c_send.at[dr], c_recv.at[dr], (r + dr) % n_row, c)

    for dr in range(1, n_row):
        c_copy(dr).start()
    cpan_ref[:, :, part(r)] = b_ref[...]

    wanted = [c * block_cols + k for k in range(block_cols)]
    wanted += [r * block_rows + k for k in range(block_rows)]

    def look(p, found):
        at, holder = perm_ref[p], p // held
        return tuple(jnp.where(at == w, holder, f) for w, f in zip(wanted, found))

    holders = lax.fori_loop(
        0, perm_ref.shape[0], look, tuple(jnp.int32(0) for _ in wanted)
    )
    for k, value in enumerate(holders):
        table_ref[k] = value

    keep_cols = pltpu.make_async_copy(cols_ref, cols_hbm, loc.at[2])

    def factor_columns():
        for dr in range(1, n_row):
            c_copy(dr, (r + n_row - dr) % n_row).wait_recv()
        step = 4 if block_cols % 4 == 0 else 1
        for w in range(0, block_cols, step):
            left = jnp.concatenate([cpan_ref[holders[w + k]] for k in range(step)], axis=0)
            done = times_inverse(left, d_ref[...]).astype(jnp.bfloat16)
            cols_ref[w * BLK:(w + step) * BLK, :] = done
        keep_cols.start()

    for d in range(1, n_pos):
        if d == n_pos - 1:
            factor_columns()

        for q in range(gpr):
            @pl.when(pos - d >= 0)
            def _(d=d, q=q):
                slot = (pos - d) * 2 + core
                remote(own_ref.at[q], rows_ref.at[slot, q], up_send.at[d - 1, q],
                       up_recv.at[d - 1, q], r, sibling).wait_recv()
                if d < n_pos - 1:
                    @pl.when(pos < n_pos - 1)
                    def _():
                        up_copy(d, q).start()
                side_copy(pos - d, q, False).start()

            @pl.when(pos + d <= n_pos - 1)
            def _(d=d, q=q):
                slot = (pos + d) * 2 + core
                remote(own_ref.at[q], rows_ref.at[slot, q], down_send.at[d - 1, q],
                       down_recv.at[d - 1, q], r, sibling).wait_recv()
                if d < n_pos - 1:
                    @pl.when(pos > 0)
                    def _():
                        down_copy(d, q).start()
                side_copy(pos + d, q, False).start()

    for dr in range(1, n_row):
        for q in range(gpr):
            a_copy(dr, q).wait_send()
        c_copy(dr).wait_send()
    for dc in range(1, n_col):
        b_copy(dc).wait_send()
    for q in range(gpr):
        for d in range(n_pos - 1):
            @pl.when((pos - d >= 0) & (pos < n_pos - 1))
            def _(d=d, q=q):
                up_copy(d, q).wait_send()

            @pl.when((pos + d <= n_pos - 1) & (pos > 0))
            def _(d=d, q=q):
                down_copy(d, q).wait_send()
        for source in range(n_pos):
            slot = source * 2 + (1 - core)
            remote(own_ref.at[q], rows_ref.at[slot, q], f_send.at[source, q],
                   f_recv.at[source, q], r, sibling).wait_recv()
            side_copy(source, q, True).wait_send()
    keep.wait()
    keep_cols.wait()


def update_kernel(tile, table, pat_ref, *refs):
    row_refs, (cols_ref, schur_ref, out_ref) = refs[:tile], refs[tile:]
    i = pl.program_id(0)
    left = jnp.concatenate([ref[0, 0] for ref in row_refs], axis=0)
    update = times_inverse(left, cols_ref[...])
    for e in range(tile):
        rows = slice(e * BLK, (e + 1) * BLK)
        for w in range(cols_ref.shape[0] // BLK):
            at = slice(w * BLK, (w + 1) * BLK)
            weight = pat_ref[w, tile * i + e].astype(jnp.float32)
            out_ref[rows, at] = schur_ref[rows, at] - update[rows, at] * weight


def local(schur, panel_raw, diag_inverse, perm, pattern):
    n_row = lax.axis_size("row")
    n_col = lax.axis_size("col")
    r = lax.axis_index("row")
    c = lax.axis_index("col")
    local_rows, local_cols = schur.shape
    block_rows, block_cols = local_rows // BLK, local_cols // BLK
    gpr = local_rows // local_cols
    held, kw = panel_raw.shape[0] // BLK, panel_raw.shape[1]
    snw = diag_inverse.shape[0]
    blocks = perm.shape[0]
    bf16 = jnp.bfloat16

    n_pos = n_col // 2
    dma = pltpu.SemaphoreType.DMA
    smem = pl.BlockSpec(memory_space=pltpu.SMEM)
    hbm = pl.BlockSpec(memory_space=pltpu.HBM)
    rows, cols, table = pl.pallas_call(
        functools.partial(exchange_kernel, n_row, n_col, gpr, held, block_cols, block_rows),
        out_shape=(
            jax.ShapeDtypeStruct((n_col, gpr, BLK, snw), bf16),
            jax.ShapeDtypeStruct((local_cols, snw), bf16),
            jax.ShapeDtypeStruct((block_cols + block_rows,), jnp.int32),
        ),
        in_specs=[smem, hbm, hbm],
        out_specs=(
            pl.BlockSpec(memory_space=pl.ANY),
            pl.BlockSpec(memory_space=pl.ANY),
            smem,
        ),
        scratch_shapes=[
            pltpu.VMEM((held, BLK, kw), bf16),
            pltpu.VMEM((n_col, BLK, kw), bf16),
            pltpu.VMEM((gpr, BLK, snw), bf16),
            pltpu.VMEM((n_col, BLK, kw), bf16),
            pltpu.VMEM((gpr, BLK, snw), bf16),
            pltpu.VMEM((snw, snw), bf16),
            pltpu.VMEM((n_col, BLK, snw), bf16),
            pltpu.VMEM((local_cols, snw), bf16),
            dma((n_row, gpr)), dma((n_row, gpr)), dma((n_col,)), dma((n_col,)),
            dma((n_row,)), dma((n_row,)), dma((n_pos, gpr)), dma((n_pos, gpr)),
            dma((n_pos, gpr)), dma((n_pos, gpr)), dma((n_pos, gpr)), dma((n_pos, gpr)), dma((4,)),
        ],
        compiler_params=pltpu.CompilerParams(
            collective_id=0, has_side_effects=True, vmem_limit_bytes=20 * 2**20
        ),
        cost_estimate=pl.CostEstimate(
            flops=2 * (local_cols + gpr * BLK) * snw * snw,
            bytes_accessed=30 * local_rows * snw,
            transcendentals=0,
        ),
    )(perm, panel_raw.reshape(held, BLK, kw), diag_inverse)

    tile = 4 if block_rows % 4 == 0 else 1

    def row_spec(e):
        return pl.BlockSpec(
            (1, 1, BLK, snw),
            lambda i, t, p: (t[block_cols + tile * i + e], (tile * i + e) // block_cols, 0, 0),
        )

    wide = pl.BlockSpec((tile * BLK, local_cols), lambda i, t, p: (i, 0))
    return pl.pallas_call(
        functools.partial(update_kernel, tile),
        out_shape=jax.ShapeDtypeStruct(schur.shape, schur.dtype),
        grid_spec=pltpu.PrefetchScalarGridSpec(
            num_scalar_prefetch=2,
            grid=(block_rows // tile,),
            in_specs=[row_spec(e) for e in range(tile)]
            + [pl.BlockSpec((local_cols, snw), lambda i, t, p: (0, 0)), wide],
            out_specs=wide,
        ),
        compiler_params=pltpu.CompilerParams(vmem_limit_bytes=28 * 2**20),
    )(table, pattern.T, *([rows] * tile), cols, schur)


def solution(mesh):
    return jax.shard_map(
        local,
        mesh=mesh,
        in_specs=(P("row", "col"), P("col", "row"), P(), P(), P("row", "col")),
        out_specs=P("row", "col"),
        check_vma=False,
    )
```

```python
import functools

import jax
import jax.numpy as jnp
from jax import lax
from jax.experimental import pallas as pl
from jax.experimental.pallas import tpu as pltpu
from jax.sharding import PartitionSpec as P

BLK = 128
MESH = pl.DeviceIdType.MESH


def times_inverse(left, right):
    return lax.dot_general(
        left, right, (((1,), (1,)), ((), ())), preferred_element_type=jnp.float32
    )


def factor(left, d_ref):
    size = d_ref.shape[0]
    step = min(256, size)
    parts = [
        times_inverse(left[:, :k + step], d_ref[k:k + step, :k + step])
        for k in range(0, size, step)
    ]
    return jnp.concatenate(parts, axis=1).astype(jnp.bfloat16)


def exchange_kernel(
    n_row, n_col, gpr, held, block_cols, block_rows,
    perm_ref, raw_hbm, d_hbm, rows_ref, cols_hbm, table_ref,
    raw_ref, sorted_ref, a_ref, b_ref, own_ref, d_ref, cpan_ref, cols_ref,
    a_send, a_recv, b_send, b_recv, c_send, c_recv,
    up_send, up_recv, down_send, down_recv, f_send, f_recv, loc,
):
    r = lax.axis_index("row")
    c = lax.axis_index("col")
    n_pos = n_col // 2
    pos = c // 2
    core = c % 2
    sibling = pos * 2 + (1 - core)
    kw = raw_ref.shape[2]
    snw = d_ref.shape[0]
    load_raw = pltpu.make_async_copy(raw_hbm, raw_ref, loc.at[3])
    load_raw.start()
    load_d = pltpu.make_async_copy(d_hbm, d_ref, loc.at[0])
    load_d.start()

    def remote(src, dst, ssem, rsem, rr, cc):
        return pltpu.make_async_remote_copy(
            src_ref=src, dst_ref=dst, send_sem=ssem, recv_sem=rsem,
            device_id=(rr, cc), device_id_type=MESH,
        )

    def part(index):
        return pl.ds(pl.multiple_of(index * kw, kw), kw)

    barrier = pltpu.get_barrier_semaphore()
    for dr in range(1, n_row):
        pl.semaphore_signal(barrier, inc=1, device_id=((r + dr) % n_row, c), device_id_type=MESH)
    for dc in range(1, n_col):
        pl.semaphore_signal(barrier, inc=1, device_id=(r, (c + dc) % n_col), device_id_type=MESH)
    groups = [lax.div(perm_ref[c * held + i], block_cols) for i in range(held)]
    load_raw.wait()
    for g in range(n_col):
        block = 0
        for i in range(1, held):
            block = jnp.where(groups[i] == g, i, block)
        sorted_ref[g] = raw_ref[block]
    pl.semaphore_wait(barrier, n_row + n_col - 2)

    def a_copy(dr, q, came=None):
        to = (r + dr) % n_row
        return remote(sorted_ref.at[to * gpr + q],
                      a_ref.at[q, :, part(r if came is None else came)],
                      a_send.at[dr, q], a_recv.at[dr, q], to, c)

    def b_copy(dc, came=None):
        to = (c + dc) % n_col
        return remote(sorted_ref.at[to], b_ref.at[c if came is None else came],
                      b_send.at[dc], b_recv.at[dc], r, to)

    for q in range(gpr):
        for dr in range(1, n_row):
            a_copy(dr, q).start()
    for dc in range(1, n_col):
        b_copy(dc).start()
    a_ref[:, :, part(r)] = sorted_ref[pl.ds(r * gpr, gpr)]
    b_ref[c] = sorted_ref[c]
    load_d.wait()
    def up_copy(d, q):
        slot = (pos - d) * 2 + core
        return remote(own_ref.at[q] if d == 0 else rows_ref.at[slot, q], rows_ref.at[slot, q],
                      up_send.at[d, q], up_recv.at[d, q], r, (pos + 1) * 2 + core)

    def down_copy(d, q):
        slot = (pos + d) * 2 + core
        return remote(own_ref.at[q] if d == 0 else rows_ref.at[slot, q], rows_ref.at[slot, q],
                      down_send.at[d, q], down_recv.at[d, q], r, (pos - 1) * 2 + core)

    def side_copy(source, q, mine):
        slot = source * 2 + core
        return remote(own_ref.at[q] if mine else rows_ref.at[slot, q], rows_ref.at[slot, q],
                      f_send.at[source, q], f_recv.at[source, q], r, sibling)

    for q in range(gpr):
        for dr in range(1, n_row):
            a_copy(dr, q, (r + n_row - dr) % n_row).wait_recv()
        own_ref[q] = factor(a_ref[q], d_ref)

        @pl.when(pos < n_pos - 1)
        def _(q=q):
            up_copy(0, q).start()

        @pl.when(pos > 0)
        def _(q=q):
            down_copy(0, q).start()

    for q in range(gpr):
        side_copy(pos, q, True).start()
    keep = pltpu.make_async_copy(own_ref, rows_ref.at[c], loc.at[1])
    keep.start()

    for dc in range(1, n_col):
        b_copy(dc, (c + n_col - dc) % n_col).wait_recv()

    def c_copy(dr, came=None):
        return remote(b_ref, cpan_ref.at[:, :, part(r if came is None else came)],
                      c_send.at[dr], c_recv.at[dr], (r + dr) % n_row, c)

    for dr in range(1, n_row):
        c_copy(dr).start()
    cpan_ref[:, :, part(r)] = b_ref[...]

    wanted = [c * block_cols + k for k in range(block_cols)]
    wanted += [r * block_rows + k for k in range(block_rows)]

    def look(p, found):
        at, holder = perm_ref[p], p // held
        return tuple(jnp.where(at == w, holder, f) for w, f in zip(wanted, found))

    holders = lax.fori_loop(
        0, perm_ref.shape[0], look, tuple(jnp.int32(0) for _ in wanted)
    )
    for k, value in enumerate(holders):
        table_ref[k] = value

    keep_cols = pltpu.make_async_copy(cols_ref, cols_hbm, loc.at[2])

    def factor_columns():
        for dr in range(1, n_row):
            c_copy(dr, (r + n_row - dr) % n_row).wait_recv()
        step = 4 if block_cols % 4 == 0 else 1
        for w in range(0, block_cols, step):
            left = jnp.concatenate([cpan_ref[holders[w + k]] for k in range(step)], axis=0)
            done = factor(left, d_ref)
            cols_ref[w * BLK:(w + step) * BLK, :] = done
        keep_cols.start()

    for d in range(1, n_pos):
        if d == n_pos - 1:
            factor_columns()

        for q in range(gpr):
            @pl.when(pos - d >= 0)
            def _(d=d, q=q):
                slot = (pos - d) * 2 + core
                remote(own_ref.at[q], rows_ref.at[slot, q], up_send.at[d - 1, q],
                       up_recv.at[d - 1, q], r, sibling).wait_recv()
                if d < n_pos - 1:
                    @pl.when(pos < n_pos - 1)
                    def _():
                        up_copy(d, q).start()
                side_copy(pos - d, q, False).start()

            @pl.when(pos + d <= n_pos - 1)
            def _(d=d, q=q):
                slot = (pos + d) * 2 + core
                remote(own_ref.at[q], rows_ref.at[slot, q], down_send.at[d - 1, q],
                       down_recv.at[d - 1, q], r, sibling).wait_recv()
                if d < n_pos - 1:
                    @pl.when(pos > 0)
                    def _():
                        down_copy(d, q).start()
                side_copy(pos + d, q, False).start()

    for dr in range(1, n_row):
        for q in range(gpr):
            a_copy(dr, q).wait_send()
        c_copy(dr).wait_send()
    for dc in range(1, n_col):
        b_copy(dc).wait_send()
    for q in range(gpr):
        for d in range(n_pos - 1):
            @pl.when((pos - d >= 0) & (pos < n_pos - 1))
            def _(d=d, q=q):
                up_copy(d, q).wait_send()

            @pl.when((pos + d <= n_pos - 1) & (pos > 0))
            def _(d=d, q=q):
                down_copy(d, q).wait_send()
        for source in range(n_pos):
            slot = source * 2 + (1 - core)
            remote(own_ref.at[q], rows_ref.at[slot, q], f_send.at[source, q],
                   f_recv.at[source, q], r, sibling).wait_recv()
            side_copy(source, q, True).wait_send()
    keep.wait()
    keep_cols.wait()


def update_kernel(tile, table, pat_ref, *refs):
    row_refs, (cols_ref, schur_ref, out_ref) = refs[:tile], refs[tile:]
    i = pl.program_id(0)
    left = jnp.concatenate([ref[0, 0] for ref in row_refs], axis=0)
    update = times_inverse(left, cols_ref[...])
    for e in range(tile):
        rows = slice(e * BLK, (e + 1) * BLK)
        for w in range(cols_ref.shape[0] // BLK):
            at = slice(w * BLK, (w + 1) * BLK)
            weight = pat_ref[w, tile * i + e].astype(jnp.float32)
            out_ref[rows, at] = schur_ref[rows, at] - update[rows, at] * weight


def local(schur, panel_raw, diag_inverse, perm, pattern):
    n_row = lax.axis_size("row")
    n_col = lax.axis_size("col")
    r = lax.axis_index("row")
    c = lax.axis_index("col")
    local_rows, local_cols = schur.shape
    block_rows, block_cols = local_rows // BLK, local_cols // BLK
    gpr = local_rows // local_cols
    held, kw = panel_raw.shape[0] // BLK, panel_raw.shape[1]
    snw = diag_inverse.shape[0]
    blocks = perm.shape[0]
    bf16 = jnp.bfloat16

    n_pos = n_col // 2
    dma = pltpu.SemaphoreType.DMA
    smem = pl.BlockSpec(memory_space=pltpu.SMEM)
    hbm = pl.BlockSpec(memory_space=pltpu.HBM)
    rows, cols, table = pl.pallas_call(
        functools.partial(exchange_kernel, n_row, n_col, gpr, held, block_cols, block_rows),
        out_shape=(
            jax.ShapeDtypeStruct((n_col, gpr, BLK, snw), bf16),
            jax.ShapeDtypeStruct((local_cols, snw), bf16),
            jax.ShapeDtypeStruct((block_cols + block_rows,), jnp.int32),
        ),
        in_specs=[smem, hbm, hbm],
        out_specs=(
            pl.BlockSpec(memory_space=pl.ANY),
            pl.BlockSpec(memory_space=pl.ANY),
            smem,
        ),
        scratch_shapes=[
            pltpu.VMEM((held, BLK, kw), bf16),
            pltpu.VMEM((n_col, BLK, kw), bf16),
            pltpu.VMEM((gpr, BLK, snw), bf16),
            pltpu.VMEM((n_col, BLK, kw), bf16),
            pltpu.VMEM((gpr, BLK, snw), bf16),
            pltpu.VMEM((snw, snw), bf16),
            pltpu.VMEM((n_col, BLK, snw), bf16),
            pltpu.VMEM((local_cols, snw), bf16),
            dma((n_row, gpr)), dma((n_row, gpr)), dma((n_col,)), dma((n_col,)),
            dma((n_row,)), dma((n_row,)), dma((n_pos, gpr)), dma((n_pos, gpr)),
            dma((n_pos, gpr)), dma((n_pos, gpr)), dma((n_pos, gpr)), dma((n_pos, gpr)), dma((4,)),
        ],
        compiler_params=pltpu.CompilerParams(
            collective_id=0, has_side_effects=True, vmem_limit_bytes=20 * 2**20
        ),
        cost_estimate=pl.CostEstimate(
            flops=2 * (local_cols + gpr * BLK) * snw * snw,
            bytes_accessed=30 * local_rows * snw,
            transcendentals=0,
        ),
    )(perm, panel_raw.reshape(held, BLK, kw), diag_inverse)

    tile = 4 if block_rows % 4 == 0 else 1

    def row_spec(e):
        return pl.BlockSpec(
            (1, 1, BLK, snw),
            lambda i, t, p: (t[block_cols + tile * i + e], (tile * i + e) // block_cols, 0, 0),
        )

    wide = pl.BlockSpec((tile * BLK, local_cols), lambda i, t, p: (i, 0))
    return pl.pallas_call(
        functools.partial(update_kernel, tile),
        out_shape=jax.ShapeDtypeStruct(schur.shape, schur.dtype),
        grid_spec=pltpu.PrefetchScalarGridSpec(
            num_scalar_prefetch=2,
            grid=(block_rows // tile,),
            in_specs=[row_spec(e) for e in range(tile)]
            + [pl.BlockSpec((local_cols, snw), lambda i, t, p: (0, 0)), wide],
            out_specs=wide,
        ),
        compiler_params=pltpu.CompilerParams(vmem_limit_bytes=28 * 2**20),
    )(table, pattern.T, *([rows] * tile), cols, schur)


def solution(mesh):
    return jax.shard_map(
        local,
        mesh=mesh,
        in_specs=(P("row", "col"), P("col", "row"), P(), P(), P("row", "col")),
        out_specs=P("row", "col"),
        check_vma=False,
    )
```
